32 devices in a mesh: tm: 4 (over x, core), row: 2 (over y), col: 4 (over z).
Axes of the slice: x: 2, y: 2, z: 4, core: 2. Of those that a mesh axis runs over, the one named last changes fastest.
Arguments:
- first_inverse: bfloat16 [4, 1536, 1536], P('tm', ('row', 'col')), as said below
- second_diag: bfloat16 [4, 1536, 1536], P('tm', ('row', 'col')), as said below
- coupling: bfloat16 [4, 3, 1536, 1536], P('tm', None, ('row', 'col'))
- arrow_rows: float32 [4, 2, 8, 1536], P('tm')
- tip_block: float32 [8, 8], replicated, may hold values from -6 to 6
Outputs:
- separator_update: float32 [4, 1536, 1536], P('tm', ('row', 'col'))
- separator_fill: float32 [4, 1536, 1536], P('tm', ('row', 'col'))
- reduced_tip: float32 [8, 8], replicated
The draws below stay inside these ranges and needn't reach their ends.
Inputs may be any that keep to these rules, and one draw needn't show every extreme that they name: For every p, first_inverse[p] is lower triangular with a positive diagonal. For every p, second_diag[p] is symmetric, and second_diag[p] minus coupling[p, 1] first_inverse[p]^T first_inverse[p] coupling[p, 1]^T is positive definite.
All inputs are finite; a program needn't handle non-finite values.
Results may differ from the reference program's by a relative error of at most 0.009.
Values may be sent and summed in bfloat16 or wider, within the bound.
No kernel may reach another device: no remote copies, remote signals or barrier semaphores. Data moves between devices by JAX's collectives and lax.ppermute only.
A program may use at most 128 MiB of HBM per device.

```python
import math
import jax
import jax.numpy as jnp
from jax import lax

NODES = 1536
FIXED = 8
PARTS_SIZE = 4


def draw_first_inverse(key, part):
    base_key = jax.random.fold_in(key, 41)
    key_diag = jax.random.fold_in(base_key, 1)
    key_off = jax.random.fold_in(base_key, 2)
    limit_value = 0.25 * math.sqrt(3.0 / NODES)
    diagonal = jax.random.uniform(key_diag, (PARTS_SIZE, NODES), jnp.float32, 0.45, 0.6)
    offdiag = jax.random.uniform(key_off, (PARTS_SIZE, NODES, NODES), jnp.float32, -limit_value, limit_value)
    rows_index = jnp.arange(NODES)[:, None]
    cols_index = jnp.arange(NODES)[None, :]
    below = (rows_index > cols_index).astype(jnp.float32)
    identity = jnp.eye(NODES, dtype=jnp.float32)
    whole = offdiag * below + identity * diagonal[..., None]
    return whole.astype(jnp.bfloat16)


def draw_second_diag(key, part):
    base_key = jax.random.fold_in(key, 11)
    key_diag = jax.random.fold_in(base_key, 1)
    key_pos = jax.random.fold_in(base_key, 2)
    key_scale = jax.random.fold_in(base_key, 3)
    leading = (PARTS_SIZE,)
    spacing = 4.0 / math.sqrt(NODES)
    places = jax.random.uniform(key_pos, leading + (NODES, 2), jnp.float32)
    diagonal = jax.random.uniform(key_diag, leading + (NODES,), jnp.float32, 3.0, 4.0)
    node_scale = jax.random.uniform(key_scale, leading + (NODES,), jnp.float32, 0.7, 1.3)
    first_gap = jnp.abs(places[..., :, None, 0] - places[..., None, :, 0])
    second_gap = jnp.abs(places[..., :, None, 1] - places[..., None, :, 1])
    kernel = jnp.exp(-(first_gap + second_gap) / spacing)
    kernel = kernel * node_scale[..., :, None] * node_scale[..., None, :]
    identity = jnp.eye(NODES, dtype=jnp.float32)
    whole = kernel + identity * diagonal[..., None]
    return whole.astype(jnp.bfloat16)


def coupling_slice(key, lowest, highest, limit_value):
    key_diag, key_off = jax.random.split(key)
    magnitude = jax.random.uniform(key_diag, (PARTS_SIZE, NODES), jnp.float32, lowest, highest)
    offdiag = jax.random.uniform(key_off, (PARTS_SIZE, NODES, NODES), jnp.float32, -limit_value, limit_value)
    identity = jnp.eye(NODES, dtype=jnp.float32)
    return offdiag * (1.0 - identity) - identity * magnitude[..., None]


def draw_coupling(key, part):
    key_top = jax.random.fold_in(key, 21)
    key_mid = jax.random.fold_in(key, 22)
    key_low = jax.random.fold_in(key, 23)
    unit_limit = math.sqrt(3.0 / NODES)
    top_slice = coupling_slice(key_top, 1.6, 2.4, 0.8 * unit_limit)
    mid_slice = coupling_slice(key_mid, 0.6, 0.9, 0.3 * unit_limit)
    low_slice = coupling_slice(key_low, 1.6, 2.4, 0.8 * unit_limit)
    return jnp.stack([top_slice, mid_slice, low_slice], axis=1).astype(jnp.bfloat16)


def draw_arrow_rows(key, part):
    key_vals = jax.random.fold_in(key, 31)
    position = jnp.arange(PARTS_SIZE, dtype=jnp.float32) / (PARTS_SIZE - 1)
    spread = 0.6 / math.sqrt(NODES)
    values = jax.random.normal(key_vals, (PARTS_SIZE, 2, FIXED, NODES), jnp.float32)
    growth = jnp.power(1.7320508, position)
    return values * spread * growth[:, None, None, None]


def normal_values(own_key, dims, scale, most, kind=jnp.bfloat16):
    return jnp.clip(scale * jax.random.normal(own_key, dims, jnp.float32), -most, most).astype(kind)


def setup_inputs(seed: int = 0) -> dict:
    streams_of = jax.random.split(jax.random.key(seed), 6)
    return {
        "first_inverse": draw_first_inverse(jax.random.fold_in(streams_of[5], 71), 0),
        "second_diag": draw_second_diag(jax.random.fold_in(streams_of[5], 71), 0),
        "coupling": draw_coupling(jax.random.fold_in(streams_of[5], 71), 0),
        "arrow_rows": draw_arrow_rows(jax.random.fold_in(streams_of[5], 71), 0),
        "tip_block": normal_values(streams_of[4], (FIXED, FIXED), 1.0, 6.0, jnp.float32),
    }


def lower_solve(factor, rhs_block):
    return lax.linalg.triangular_solve(factor, rhs_block, left_side=True, lower=True)

def partition(blocks):
    inverse_one, second_diag, coupling_set, arrow_pair = blocks
    top_panel = jnp.dot(inverse_one.astype(jnp.float32), coupling_set[0].T.astype(jnp.float32), preferred_element_type=jnp.float32).astype(jnp.bfloat16)
    mid_panel = jnp.dot(inverse_one.astype(jnp.float32), coupling_set[1].T.astype(jnp.float32), preferred_element_type=jnp.float32).astype(jnp.bfloat16)
    arrow_one = jnp.dot(inverse_one.astype(jnp.float32), arrow_pair[0].T, precision=lax.Precision.HIGHEST)
    sep_first = jnp.dot(top_panel.T.astype(jnp.float32), top_panel.astype(jnp.float32), preferred_element_type=jnp.float32)
    second_block = (second_diag.astype(jnp.float32) - jnp.dot(mid_panel.T.astype(jnp.float32), mid_panel.astype(jnp.float32), preferred_element_type=jnp.float32)).astype(jnp.bfloat16)
    fill_cols = -jnp.dot(mid_panel.T.astype(jnp.float32), top_panel.astype(jnp.float32), preferred_element_type=jnp.float32)
    arrow_two_rows = arrow_pair[1] - jnp.dot(arrow_one.T.astype(jnp.bfloat16).astype(jnp.float32), mid_panel.astype(jnp.float32), preferred_element_type=jnp.float32)
    tip_first = jnp.dot(arrow_one.T.astype(jnp.float32), arrow_one.astype(jnp.float32), preferred_element_type=jnp.float32, precision=lax.Precision.HIGHEST)
    factor_two = jnp.linalg.cholesky(second_block.astype(jnp.float32))
    upper_panel = lower_solve(factor_two, fill_cols).astype(jnp.bfloat16)
    lower_panel = lower_solve(factor_two, coupling_set[2].T.astype(jnp.float32)).astype(jnp.bfloat16)
    arrow_two = lower_solve(factor_two, arrow_two_rows.T)
    sep_second = jnp.dot(upper_panel.T.astype(jnp.float32), upper_panel.astype(jnp.float32), preferred_element_type=jnp.float32)
    fill_block = -jnp.dot(upper_panel.T.astype(jnp.float32), lower_panel.astype(jnp.float32), preferred_element_type=jnp.float32)
    handed = jnp.dot(lower_panel.T.astype(jnp.float32), lower_panel.astype(jnp.float32), preferred_element_type=jnp.float32)
    tip_second = jnp.dot(arrow_two.T.astype(jnp.float32), arrow_two.astype(jnp.float32), preferred_element_type=jnp.float32, precision=lax.Precision.HIGHEST)
    return (sep_first + sep_second, fill_block, handed, tip_first + tip_second)

def reference(first_inverse, second_diag, coupling, arrow_rows, tip_block):
    own_update, fill_block, handed, tip_terms = lax.map(partition, (first_inverse, second_diag, coupling, arrow_rows))
    incoming = jnp.concatenate([jnp.zeros_like(handed[:1]), handed[:-1]], axis=0)
    return (own_update + incoming, fill_block, tip_block - jnp.sum(tip_terms, axis=0))
```

```python
import functools
import jax
import jax.numpy as jnp
from jax import lax
from jax.experimental import pallas as pl
from jax.experimental.pallas import tpu as pltpu
from jax.sharding import PartitionSpec as P

F32, BF16 = jnp.float32, jnp.bfloat16
NT = (((1,), (1,)), ((), ()))
NN = (((1,), (0,)), ((), ()))

def mm(a, b, dims=NN):
    return lax.dot_general(a, b, dims, preferred_element_type=F32)

def split(a):
    hi = a.astype(BF16)
    return hi, (a - hi.astype(F32)).astype(BF16)

def mm3(a, b):
    return mm(a[0], b[0]) + (mm(a[0], b[1]) + mm(a[1], b[0]))

def spd_inverse(block, quick):
    size = block.shape[0]
    eye = (lax.broadcasted_iota(jnp.int32, (size, size), 0)
           == lax.broadcasted_iota(jnp.int32, (size, size), 1)).astype(F32)
    start = eye / jnp.sum(jnp.abs(block), axis=0, keepdims=True)
    parts = split(block)
    guess = start
    for _ in range(quick):
        short = guess.astype(BF16)
        guess = 2.0 * guess - mm(short, mm(parts[0], short).astype(BF16))
    def gap_of(x):
        gap = eye - mm3(parts, split(x))
        return gap, jnp.max(jnp.sum(jnp.abs(gap), axis=0, keepdims=True))
    gap, worst = gap_of(guess)
    good = worst < 0.5
    guess = jnp.where(good, guess, start)
    def go(state):
        turn, worst, _ = state
        return jnp.logical_and(turn < 60, worst > 2e-2)
    def step(state):
        turn, worst, x = state
        gap, _ = gap_of(x)
        x = x + mm3(split(x), split(gap))
        _, worst = gap_of(x)
        return turn + 1, worst, x
    _, _, guess = lax.while_loop(go, step, (0, jnp.where(good, worst, 1.0), guess))
    gap, _ = gap_of(guess)
    return guess + mm3(split(guess), split(gap))

def eliminate_kernel(size, quick, s_in, r_in, g_ref, s_ref, r_ref, low_ref):
    n = s_in.shape[0]
    nb = n // size
    s_ref[...] = s_in[...]
    r_ref[...] = r_in[...]
    at = lambda k: pl.ds(k * size, size)
    for k in range(nb):
        inverse = spd_inverse(s_ref[at(k), at(k)], quick).astype(BF16)
        row = r_ref[:, at(k)].astype(BF16)
        g_ref[:, at(k)] = mm(row, inverse)
        for j in range(k + 1, nb):
            low_ref[at(j), at(k)] = mm(s_ref[at(j), at(k)].astype(BF16), inverse).astype(BF16)
        for j in range(k + 1, nb):
            low = low_ref[at(j), at(k)]
            r_ref[:, at(j)] -= mm(row, low, NT)
            for i in range(j, nb):
                s_ref[at(i), at(j)] -= mm(s_ref[at(i), at(k)].astype(BF16), low, NT)
    for k in range(nb - 2, -1, -1):
        rest = pl.ds((k + 1) * size, n - (k + 1) * size)
        g_ref[:, at(k)] -= mm(g_ref[:, rest].astype(BF16), low_ref[rest, at(k)])

def eliminate(block, rows, size=256, quick=4):
    n, r = block.shape[0], rows.shape[0]
    v = pl.BlockSpec(memory_space=pltpu.VMEM)
    return pl.pallas_call(
        functools.partial(eliminate_kernel, size, quick),
        out_shape=jax.ShapeDtypeStruct((r, n), F32),
        in_specs=[v, v], out_specs=v,
        scratch_shapes=[pltpu.VMEM((n, n), F32), pltpu.VMEM((r, n), F32), pltpu.VMEM((n, n), BF16)],
        compiler_params=pltpu.CompilerParams(vmem_limit_bytes=60 << 20),
        cost_estimate=pl.CostEstimate(flops=2 * n**3, bytes_accessed=4 * n * n + 8 * n * r, transcendentals=0),
        name="eliminate",
    )(block, rows)


def from_behind(block, axis, distance):
    devices = range(lax.axis_size(axis))
    route = [(i - distance, i) for i in devices if i - distance in devices]
    return lax.ppermute(block, axis, route)


def gather_block(one_share):
    return lax.all_gather(one_share, ("row", "col"), axis=0, tiled=True)


def shards(first_inverse, second_diag, coupling, arrow_rows, tip_block):
    share, n = coupling.shape[2:]
    size = 256 if n % 256 == 0 else 128
    top_share, mid_share, low_share = (coupling[0, i] for i in range(3))
    inverse = gather_block(first_inverse[0])
    mid_rhs = gather_block(mid_share)
    diag = gather_block(second_diag[0])
    top_rhs = gather_block(top_share)
    low_rhs = gather_block(low_share)
    mid = mm(mid_rhs, inverse, NT).astype(BF16)
    top_own = mm(top_share, inverse, NT).astype(BF16)
    arrow_one = jnp.einsum(
        "ik,jk->ij", arrow_rows[0, 0], inverse.astype(F32), precision=lax.Precision.HIGHEST
    )
    block = diag.astype(F32) - mm(mid, mid, NT)
    fill_rows = -mm(top_own, mid, NT)
    arrow_two_rows = arrow_rows[0, 1] - mm(arrow_one.astype(BF16), mid, NT)
    rows = jnp.concatenate([fill_rows, low_share.astype(F32), arrow_two_rows], axis=0)
    solved = eliminate(block, rows, size)
    upper = solved[:share].astype(BF16)
    lower = solved[share : 2 * share].astype(BF16)
    left = (top_own.astype(F32) - mm(upper, mid)).astype(BF16)
    own_update = mm(mm(left, inverse).astype(BF16), top_rhs, NT)
    fill_block = -mm(upper, low_rhs, NT)
    handed = mm(lower, low_rhs, NT)
    tip_terms = jnp.einsum("ik,jk->ij", arrow_one, arrow_one, precision=lax.Precision.HIGHEST)
    tip_terms += jnp.einsum(
        "ik,jk->ij", solved[2 * share :], arrow_two_rows, precision=lax.Precision.HIGHEST
    )
    incoming = from_behind(handed, "tm", 1)
    tip_total = lax.psum(tip_terms, "tm")
    return ((own_update + incoming)[None], fill_block[None], tip_block - tip_total)


def solution(mesh):
    return jax.shard_map(
        shards,
        mesh=mesh,
        in_specs=(
            P("tm", ("row", "col"), None),
            P("tm", ("row", "col"), None),
            P("tm", None, ("row", "col"), None),
            P("tm", None, None, None),
            P(),
        ),
        out_specs=(P("tm", ("row", "col"), None), P("tm", ("row", "col"), None), P()),
        check_vma=False,
    )
```

```python
import functools
import jax
import jax.numpy as jnp
from jax import lax
from jax.experimental import pallas as pl
from jax.experimental.pallas import tpu as pltpu
from jax.sharding import PartitionSpec as P

F32, BF16 = jnp.float32, jnp.bfloat16
NT = (((1,), (1,)), ((), ()))
NN = (((1,), (0,)), ((), ()))

def mm(a, b, dims=NN):
    return lax.dot_general(a, b, dims, preferred_element_type=F32)

def split(a):
    hi = a.astype(BF16)
    return hi, (a - hi.astype(F32)).astype(BF16)

def mm3(a, b):
    return mm(a[0], b[0]) + (mm(a[0], b[1]) + mm(a[1], b[0]))

def spd_inverse(block, quick):
    size = block.shape[0]
    eye = (lax.broadcasted_iota(jnp.int32, (size, size), 0)
           == lax.broadcasted_iota(jnp.int32, (size, size), 1)).astype(F32)
    start = eye / jnp.sum(jnp.abs(block), axis=0, keepdims=True)
    parts = split(block)
    guess = start
    for _ in range(quick):
        short = guess.astype(BF16)
        guess = 2.0 * guess - mm(short, mm(parts[0], short).astype(BF16))
    def gap_of(x):
        gap = eye - mm3(parts, split(x))
        return gap, jnp.max(jnp.sum(jnp.abs(gap), axis=0, keepdims=True))
    gap, worst = gap_of(guess)
    good = worst < 0.5
    guess = jnp.where(good, guess, start)
    def go(state):
        turn, worst, _ = state
        return jnp.logical_and(turn < 60, worst > 2e-2)
    def step(state):
        turn, worst, x = state
        gap, _ = gap_of(x)
        x = x + mm3(split(x), split(gap))
        _, worst = gap_of(x)
        return turn + 1, worst, x
    _, _, guess = lax.while_loop(go, step, (0, jnp.where(good, worst, 1.0), guess))
    gap, _ = gap_of(guess)
    return guess + mm3(split(guess), split(gap))

def eliminate_kernel(size, quick, s_in, r_in, g_ref, s_ref, r_ref, low_ref):
    n = s_in.shape[0]
    nb = n // size
    s_ref[...] = s_in[...]
    r_ref[...] = r_in[...]
    at = lambda k: pl.ds(k * size, size)
    for k in range(nb):
        inverse = spd_inverse(s_ref[at(k), at(k)], quick).astype(BF16)
        row = r_ref[:, at(k)].astype(BF16)
        g_ref[:, at(k)] = mm(row, inverse)
        for j in range(k + 1, nb):
            low_ref[at(j), at(k)] = mm(s_ref[at(j), at(k)].astype(BF16), inverse).astype(BF16)
        for j in range(k + 1, nb):
            low = low_ref[at(j), at(k)]
            r_ref[:, at(j)] -= mm(row, low, NT)
            for i in range(j, nb):
                s_ref[at(i), at(j)] -= mm(s_ref[at(i), at(k)].astype(BF16), low, NT)
    for k in range(nb - 2, -1, -1):
        rest = pl.ds((k + 1) * size, n - (k + 1) * size)
        g_ref[:, at(k)] -= mm(g_ref[:, rest].astype(BF16), low_ref[rest, at(k)])

def eliminate(block, rows, size=256, quick=4):
    n, r = block.shape[0], rows.shape[0]
    v = pl.BlockSpec(memory_space=pltpu.VMEM)
    return pl.pallas_call(
        functools.partial(eliminate_kernel, size, quick),
        out_shape=jax.ShapeDtypeStruct((r, n), F32),
        in_specs=[v, v], out_specs=v,
        scratch_shapes=[pltpu.VMEM((n, n), F32), pltpu.VMEM((r, n), F32), pltpu.VMEM((n, n), BF16)],
        compiler_params=pltpu.CompilerParams(vmem_limit_bytes=60 << 20),
        cost_estimate=pl.CostEstimate(flops=2 * n**3, bytes_accessed=4 * n * n + 8 * n * r, transcendentals=0),
        name="eliminate",
    )(block, rows)


AXES = ("tm", "row", "col")


def places():
    tms, rows, cols = (lax.axis_size(a) for a in AXES)
    flat = lambda t, r, c: (t * rows + r) * cols + c
    return [(t, r, c) for t in range(tms) for r in range(rows) for c in range(cols)], flat, rows, cols


def move(block, target):
    devices, flat, _, _ = places()
    route = [(flat(*d), flat(*target(*d))) for d in devices if target(*d) is not None]
    return lax.ppermute(block, AXES, route)


def swapped(t, r, c):
    half = lax.axis_size("col") // 2
    if t % 2 == c // half:
        return t, r, c
    return t ^ 1, r, (c + half) % (2 * half)


def along(axis, step):
    def target(t, r, c):
        rows, half = lax.axis_size("row"), lax.axis_size("col") // 2
        if axis == "core":
            return t ^ 1, r, c
        if axis == "row":
            return t, (r + step) % rows, c
        return t, r, c // half * half + (c % half + step) % half
    return target


def after(value, *others):
    return lax.optimization_barrier((value, *others))[0]


def spread(own):
    rows, half = lax.axis_size("row"), lax.axis_size("col") // 2
    if rows == 2 and half == 2:
        by_row = move(own, along("row", 1))
        by_col = move(own, along("col", 1))
        cut = own.shape[0] * 3 // 4 // 16 * 16
        first = move(by_col[:cut], along("row", 1))
        second = move(by_row[cut:], along("col", 1))
        return [(0, 0, 0, own), (1, 0, 0, by_row), (0, 1, 0, by_col), (1, 1, 0, first), (1, 1, cut, second)]
    return None


def groups():
    devices, flat, rows, cols = places()
    half = cols // 2
    return [
        [flat(2 * x + core, r, h * half + c) for r in range(rows) for core in range(2) for c in range(half)]
        for x in range(lax.axis_size("tm") // 2)
        for h in range(2)
    ]


def gather(own, natural):
    share = own.shape[0]
    rows, cols = lax.axis_size("row"), lax.axis_size("col")
    half = cols // 2
    pieces = spread(own)
    if pieces is None:
        return lax.all_gather(own, AXES, axis=0, tiled=True, axis_index_groups=groups())
    pieces = [(0, *p) for p in pieces]
    pieces += [(1, j, i, k, move(block, along("core", 1))) for _, j, i, k, block in pieces]
    if not natural:
        return jnp.concatenate([p[-1] for p in pieces], axis=0)
    core = lax.axis_index("tm") % 2
    row, col = lax.axis_index("row"), lax.axis_index("col") % half
    whole = jnp.zeros((share * rows * cols,) + own.shape[1:], own.dtype)
    for s, j, i, k, block in pieces:
        index = ((row - j) % rows * 2 + (core - s) % 2) * half + (col - i) % half
        whole = lax.dynamic_update_slice(whole, block, (index * share + k, 0))
    return whole


def handed_to(t, r, c):
    tms, half = lax.axis_size("tm"), lax.axis_size("col") // 2
    part = t // 2 * 2 + c // half + 1
    return None if part >= tms else (part, r, c % half + t % 2 * half)


def thin(rows):
    terms = []
    for _ in range(3):
        terms.append(rows.astype(BF16))
        rows = rows - terms[-1].astype(F32)
    return jnp.concatenate(terms, axis=0)


def shards(first_inverse, second_diag, coupling, arrow_rows, tip_block):
    share, n = coupling.shape[2:]
    size = 256 if n % 256 == 0 else 128
    half = lax.axis_size("col") // 2
    core, col = lax.axis_index("tm") % 2, lax.axis_index("col")
    stays = core == col // half
    arrows = move(arrow_rows[0], swapped)
    inverse_own = move(first_inverse[0], swapped)
    mid_share = move(after(coupling[0, 1], inverse_own), swapped)
    inverse = gather(inverse_own, False)
    diag_share = move(after(second_diag[0], mid_share), swapped)
    mid_rhs = gather(mid_share, True)
    low_share = move(after(coupling[0, 2], diag_share), swapped)
    diag = gather(diag_share, True)
    top_share = move(after(coupling[0, 0], low_share), swapped)
    low_rhs = gather(low_share, True)
    top_rhs = gather(top_share, True)

    mid = mm(mid_rhs, inverse, NT).astype(BF16)
    fixed = arrows.shape[1]
    thin_one = mm(thin(arrows[0]), inverse, NT)
    arrow_one = thin_one[:fixed] + thin_one[fixed : 2 * fixed] + thin_one[2 * fixed :]
    top_own = mm(top_share, inverse, NT).astype(BF16)
    block = diag.astype(F32) - mm(mid, mid, NT)
    fill_rows = -mm(top_own, mid, NT)
    arrow_two_rows = arrows[1] - mm(arrow_one.astype(BF16), mid, NT)
    rows = jnp.concatenate([fill_rows, low_share.astype(F32), arrow_two_rows], axis=0)
    solved = eliminate(block, rows, size)
    upper = solved[:share].astype(BF16)
    lower = solved[share : 2 * share].astype(BF16)
    incoming = move(mm(lower, low_rhs, NT).astype(BF16), handed_to)
    fill_block = -mm(upper, low_rhs, NT)
    fill_far = move(fill_block.astype(BF16), swapped)
    left = (top_own.astype(F32) - mm(upper, mid)).astype(BF16)
    own_update = mm(mm(left, inverse).astype(BF16), top_rhs, NT)
    far_update = move(own_update.astype(BF16), swapped)
    tip_terms = jnp.einsum("ik,jk->ij", arrow_one, arrow_one, precision=lax.Precision.HIGHEST)
    tip_terms += jnp.einsum(
        "ik,jk->ij", solved[2 * share :], arrow_two_rows, precision=lax.Precision.HIGHEST
    )
    speaks = jnp.logical_and(stays, col % half == 0)
    tip_total = lax.psum(jnp.where(speaks, tip_terms, 0.0), ("tm", "col"))
    fill_block = jnp.where(stays, fill_block, fill_far.astype(F32))
    update = jnp.where(stays, own_update, far_update.astype(F32)) + incoming.astype(F32)
    return (update[None], fill_block[None], tip_block - tip_total)


def solution(mesh):
    return jax.shard_map(
        shards,
        mesh=mesh,
        in_specs=(
            P("tm", ("row", "col"), None),
            P("tm", ("row", "col"), None),
            P("tm", None, ("row", "col"), None),
            P("tm", None, None, None),
            P(),
        ),
        out_specs=(P("tm", ("row", "col"), None), P("tm", ("row", "col"), None), P()),
        check_vma=False,
    )
```

```python
import functools
import jax
import jax.numpy as jnp
from jax import lax
from jax.experimental import pallas as pl
from jax.experimental.pallas import tpu as pltpu
from jax.sharding import PartitionSpec as P

F32, BF16 = jnp.float32, jnp.bfloat16
NT = (((1,), (1,)), ((), ()))
NN = (((1,), (0,)), ((), ()))
AXES = ("tm", "row", "col")
HIGHEST = lax.Precision.HIGHEST


def native(t, c):
    return t % 2 == c // (lax.axis_size("col") // 2)


def move(block, target):
    tms, rows, cols = (lax.axis_size(a) for a in AXES)
    flat = lambda t, r, c: (t * rows + r) * cols + c
    devices = [(t, r, c) for t in range(tms) for r in range(rows) for c in range(cols)]
    route = [(flat(*d), flat(*target(*d))) for d in devices if target(*d) is not None]
    return lax.ppermute(block, AXES, route)


def swapped(t, r, c):
    cols = lax.axis_size("col")
    return (t, r, c) if native(t, c) else (t ^ 1, r, (c + cols // 2) % cols)


def by_row(t, r, c):
    return t, r ^ 1, c


def by_col(t, r, c):
    return t, r, c ^ 1


def by_core(t, r, c):
    return t ^ 1, r, c


def only(keep, target):
    return lambda t, r, c: target(t, r, c) if native(t, c) == keep else None


def swap_or_row(t, r, c):
    return (by_row if native(t, c) else swapped)(t, r, c)


def handed_to(t, r, c):
    half = lax.axis_size("col") // 2
    part = t // 2 * 2 + c // half + 1
    return None if part >= lax.axis_size("tm") else (part, r, c % half + t % 2 * half)


def groups():
    tms, rows, cols = (lax.axis_size(a) for a in AXES)
    half = cols // 2
    return [
        [((2 * x + k) * rows + r) * cols + h * half + c for r in range(rows) for k in range(2) for c in range(half)]
        for x in range(tms // 2)
        for h in range(2)
    ]


def after(value, *others):
    return lax.optimization_barrier((value, *others))[0]


def spread(top, bottom, share):
    rows, half = lax.axis_size("row"), lax.axis_size("col") // 2
    core = lax.axis_index("tm") % 2
    r, c = lax.axis_index("row"), lax.axis_index("col") % half
    stays = core == lax.axis_index("col") // half
    cut = top.shape[0]
    both = jnp.concatenate([top, bottom], axis=0)
    if rows != 2 or half != 2:
        own = move(both, swapped)
        whole = [
            lax.all_gather(x, AXES, axis=0, tiled=False, axis_index_groups=groups())
            for x in (own[:cut], own[cut:])
        ]
        pieces = [[(w[i], 0) for i in range(rows * 2 * half)] for w in whole]
        places = jnp.arange(rows * 2 * half, dtype=jnp.int32)
        return own, pieces, jnp.concatenate([places, places]), (own,)
    first = move(both, swap_or_row)
    second = move(both, only(True, by_col))
    own = jnp.where(stays, both, first)
    top_diag = move(jnp.where(stays, second[:cut], first[:cut]), by_row)
    low_diag = move(first[cut:], by_col)
    low_row = move(first[cut:], only(False, by_row))
    top_col = move(first[:cut], only(False, by_col))
    top_last = move(top_col, only(False, by_row))
    low_last = move(low_row, only(False, by_col))
    third = jnp.where(stays, both, jnp.concatenate([top_col, low_row], axis=0))
    fourth = jnp.where(stays, second, jnp.concatenate([top_last, low_last], axis=0))
    mine = [first, top_diag, low_diag, third, fourth]
    other = [move(x, by_core) for x in mine]

    def place(k, stays, when, otherwise):
        dr, dc = (jnp.where(stays, a, b) for a, b in zip(when, otherwise))
        return ((r ^ dr) * 2 + k) * half + (c ^ dc)

    moves = ((1, 0), (0, 0)), ((1, 1), (1, 0)), ((1, 1), (0, 1)), ((0, 0), (0, 1)), ((0, 0), (1, 0)), ((0, 1), (1, 1))
    order = (0, 1, 3, 5), (0, 2, 4, 5)
    places = [
        place(k, s, *moves[i]) for o in order for k, s in ((core, stays), (1 - core, ~stays)) for i in o
    ]
    tops = [(x, 0) for side in (mine, other) for x in (side[0], side[1], side[3], side[4])]
    lows = [
        (x, f) for side in (mine, other) for x, f in ((side[0], cut), (side[2], 0), (side[3], cut), (side[4], cut))
    ]
    return own, (tops, lows), jnp.stack(places).astype(jnp.int32), (top_diag, low_diag)


def mm(a, b, dims=NN, precision=None):
    return lax.dot_general(a, b, dims, preferred_element_type=F32, precision=precision)


def split(a):
    hi = a.astype(BF16)
    return hi, (a - hi.astype(F32)).astype(BF16)


def mm3(a, b):
    return mm(a[0], b[0]) + (mm(a[0], b[1]) + mm(a[1], b[0]))


def grid_of(rows, cols, first_row=0, first_col=0):
    row = lax.broadcasted_iota(jnp.int32, (rows, cols), 0) + first_row
    return row, lax.broadcasted_iota(jnp.int32, (rows, cols), 1) + first_col


def copies(firsts, share, places, offset, pieces, whole, sems):
    started = []
    for i, (first, piece) in enumerate(zip(firsts, pieces)):
        at = pl.ds(pl.multiple_of(places[offset + i] * share, 8), share)
        started.append(pltpu.make_async_copy(piece.at[pl.ds(first, share)], whole.at[at], sems.at[i]))
        started[-1].start()
    return started


def wait(started):
    for copy in started:
        copy.wait()


def keep_lower(whole, size):
    n = whole.shape[0]
    for k in range(n // size):
        rows = pl.ds(k * size, size)
        row, col = grid_of(size, n, k * size)
        whole[rows, :] = jnp.where(col <= row, whole[rows, :].astype(F32), 0.0).astype(BF16)


def middle_kernel(size, share, firsts, places, *refs):
    count = len(firsts[0])
    tops, lows = refs[:count], refs[count : 2 * count]
    mid_ref, inverse, rhs, sems = refs[2 * count :]
    one = copies(firsts[0], share, places, 0, tops, inverse, sems.at[0])
    two = copies(firsts[1], share, places, count, lows, rhs, sems.at[1])
    wait(one)
    keep_lower(inverse, size)
    wait(two)
    for k in range(mid_ref.shape[0] // size):
        rows, depth = pl.ds(k * size, size), pl.ds(0, (k + 1) * size)
        mid_ref[:, rows] = mm(rhs[:, depth], inverse[rows, depth], NT).astype(BF16)


def spd_inverse(block, quick):
    size = block.shape[0]
    row, col = grid_of(size, size)
    eye = (row == col).astype(F32)
    start = eye / jnp.sum(jnp.abs(block), axis=0, keepdims=True)
    parts = split(block)
    guess = start
    for _ in range(quick):
        short = guess.astype(BF16)
        guess = 2.0 * guess - mm(short, mm(parts[0], short).astype(BF16))

    def gap_of(x):
        gap = eye - mm3(parts, split(x))
        return gap, jnp.max(jnp.sum(jnp.abs(gap), axis=0, keepdims=True))

    _, worst = gap_of(guess)
    good = worst < 0.5
    guess = jnp.where(good, guess, start)

    def go(state):
        turn, worst, _ = state
        return jnp.logical_and(turn < 60, worst > 2e-2)

    def step(state):
        turn, _, x = state
        gap, _ = gap_of(x)
        x = x + mm3(split(x), split(gap))
        return turn + 1, gap_of(x)[1], x

    guess = lax.while_loop(go, step, (0, jnp.where(good, worst, 1.0), guess))[2]
    return guess + mm3(split(guess), split(gap_of(guess)[0]))


def factor_kernel(size, quick, share, firsts, places, mid, diag, *refs):
    count = len(firsts)
    tops = refs[:count]
    low_ref, inv_ref, packed, block, sems = refs[count:]
    started = copies(firsts, share, places, 0, tops, packed, sems)
    blocks = mid.shape[0] // size
    at = lambda k: pl.ds(k * size, size)
    wait(started)
    for k in range(blocks):
        for j in range(k, blocks):
            own = packed[at(k), at(j)].astype(F32)
            if j == k:
                row, col = grid_of(size, size)
                own = jnp.where(col > row, own, 0.0)
                own = own + own.T + jnp.where(col == row, diag[:, at(k)], 0.0)
            else:
                own = own.T
            block[at(j), at(k)] = own - mm(mid[at(j), :], mid[at(k), :], NT)
    for k in range(blocks):
        inverse = spd_inverse(block[at(k), at(k)], quick).astype(BF16)
        inv_ref[at(k), :] = inverse
        for j in range(k + 1, blocks):
            low_ref[at(j), at(k)] = mm(block[at(j), at(k)].astype(BF16), inverse).astype(BF16)
        for j in range(k + 1, blocks):
            low = low_ref[at(j), at(k)]
            for i in range(j, blocks):
                block[at(i), at(j)] -= mm(block[at(i), at(k)].astype(BF16), low, NT)


def solve_kernel(size, share, firsts, places, mid, low_ref, inv, own_top, own_low, arrows, *refs):
    count = len(firsts)
    tops = refs[:count]
    upper_ref, left_ref, tip_ref, inverse, top, rows, solved, sems = refs[count:]
    started = copies(firsts, share, places, 0, tops, inverse, sems)
    n = mid.shape[0]
    blocks, fixed = n // size, arrows.shape[0] // 2
    at = lambda k: pl.ds(k * size, size)
    wait(started)
    keep_lower(inverse, size)
    terms, rest = [], arrows[:fixed]
    for _ in range(3):
        terms.append(rest.astype(BF16).astype(F32))
        rest = rest - terms[-1]
    thin = jnp.concatenate(terms, axis=0).astype(BF16)
    arrow_parts = mm(thin, inverse[...], NT)
    arrow_one = arrow_parts[:fixed] + arrow_parts[fixed : 2 * fixed] + arrow_parts[2 * fixed :]
    for k in range(blocks):
        depth = pl.ds(0, (k + 1) * size)
        top[:, at(k)] = mm(own_top[:, depth], inverse[at(k), depth], NT).astype(BF16)
    rows[:share] = -mm(top[...], mid[...], NT)
    rows[share : 2 * share] = own_low[...].astype(F32)
    arrow_two = arrows[fixed:] - mm(arrow_one.astype(BF16), mid[...], NT)
    rows[2 * share :] = arrow_two
    for k in range(blocks):
        row = rows[:, at(k)].astype(BF16)
        solved[:, at(k)] = mm(row, inv[at(k), :])
        if k + 1 < blocks:
            rest = pl.ds((k + 1) * size, n - (k + 1) * size)
            rows[:, rest] -= mm(row, low_ref[rest, at(k)], NT)
    for k in range(blocks - 2, -1, -1):
        rest = pl.ds((k + 1) * size, n - (k + 1) * size)
        solved[:, at(k)] -= mm(solved[:, rest].astype(BF16), low_ref[rest, at(k)])
    upper_ref[...] = solved[: 2 * share].astype(BF16)
    left = (top[...].astype(F32) - mm(upper_ref[:share], mid[...])).astype(BF16)
    for k in range(blocks):
        depth = pl.ds(k * size, n - k * size)
        left_ref[:, at(k)] = mm(left[:, k * size :], inverse[depth, at(k)]).astype(BF16)
    tip_ref[...] = mm(arrow_one, arrow_one, NT, HIGHEST) + mm(solved[2 * share :], arrow_two, NT, HIGHEST)


def product_kernel(share, firsts, offset, signs, places, left, *refs):
    count = len(firsts)
    pieces = refs[:count]
    outs, (whole, sems) = refs[count:-2], refs[-2:]
    started = copies(firsts, share, places, offset, pieces, whole, sems)
    wait(started)
    for i, sign in enumerate(signs):
        product = mm(left[i * share : (i + 1) * share], whole[...], NT)
        product = product if sign > 0 else -product
        outs[2 * i][...] = product
        outs[2 * i + 1][...] = product.astype(BF16)


VMEM = pl.BlockSpec(memory_space=pltpu.VMEM)
ANY = pl.BlockSpec(memory_space=pl.ANY)
SMEM = pl.BlockSpec(memory_space=pltpu.SMEM)


def call(kernel, name, outs, places, dense, pieces, scratch, flops):
    arrays = [array for array, _ in pieces]
    size = lambda x: x.size * x.dtype.itemsize
    return pl.pallas_call(
        kernel,
        out_shape=outs,
        in_specs=[SMEM] + [VMEM] * len(dense) + [ANY] * len(arrays),
        out_specs=[VMEM] * len(outs),
        scratch_shapes=scratch,
        compiler_params=pltpu.CompilerParams(vmem_limit_bytes=60 << 20),
        cost_estimate=pl.CostEstimate(
            flops=flops, bytes_accessed=sum(map(size, [*dense, *arrays, *outs])), transcendentals=0
        ),
        name=name,
    )(places, *dense, *arrays)


def shards(first_inverse, second_diag, coupling, arrow_rows, tip_block):
    share, n = coupling.shape[2:]
    size = 256 if n % 256 == 0 else 128
    cols = lax.axis_size("col")
    half, fixed = cols // 2, arrow_rows.shape[2]
    core, col = lax.axis_index("tm") % 2, lax.axis_index("col")
    stays = core == col // half
    shape = jax.ShapeDtypeStruct
    dma = pltpu.SemaphoreType.DMA

    row, column = grid_of(share, n, (lax.axis_index("row") * cols + col) * share)
    diag_own = jnp.sum(jnp.where(row == column, second_diag[0], 0), axis=0, keepdims=True)
    packed = jnp.where(column <= row, first_inverse[0], second_diag[0])
    packed = jnp.concatenate([packed, jnp.pad(diag_own, ((0, 15), (0, 0)))], axis=0)
    arrows = move(arrow_rows[0].reshape(2 * fixed, n), swapped)
    _, (tops, lows), places, gate = spread(packed, coupling[0, 1], share)
    low_share, top_share = after(coupling[0, 2], *gate), after(coupling[0, 0], *gate)
    own, (low_pieces, top_pieces), later, _ = spread(low_share, top_share, share)
    own_low, own_top = own[:share], own[share:]
    diag = sum(array[share : share + 1].astype(F32) for array, _ in tops)

    firsts = [[f for _, f in p] for p in (tops, lows)]
    count = len(tops)
    whole = pltpu.VMEM((n, n), BF16)
    (mid,) = call(
        functools.partial(middle_kernel, size, share, firsts), "middle",
        [shape((n, n), BF16)], places, [], tops + lows, [whole, whole, dma((2, count))], n**3,
    )
    low, inverses = call(
        functools.partial(factor_kernel, size, 4, share, firsts[0]), "factor",
        [shape((n, n), BF16), shape((n, size), BF16)], places, [mid, diag], tops,
        [whole, pltpu.VMEM((n, n), F32), dma((count,))], 2 * n**3,
    )
    solved, left, tip_terms = call(
        functools.partial(solve_kernel, size, share, firsts[0]), "solve",
        [shape((2 * share, n), BF16), shape((share, n), BF16), shape((fixed, fixed), F32)],
        places, [mid, low, inverses, own_top, own_low, arrows], tops,
        [whole, pltpu.VMEM((share, n), BF16), pltpu.VMEM((2 * share + fixed, n), F32),
         pltpu.VMEM((2 * share + fixed, n), F32), dma((count,))], 8 * share * n * n,
    )
    out = [shape((share, n), F32), shape((share, n), BF16)]
    firsts = [[f for _, f in p] for p in (low_pieces, top_pieces)]
    fill_block, fill_sent, _, handed = call(
        functools.partial(product_kernel, share, firsts[0], 0, (-1, 1)), "fill",
        out + out, later, [solved], low_pieces, [whole, dma((count,))], 4 * share * n * n,
    )
    incoming = move(handed, handed_to)
    fill_far = move(fill_sent, swapped)
    own_update, update_sent = call(
        functools.partial(product_kernel, share, firsts[1], count, (1,)), "update",
        out, later, [left], top_pieces, [whole, dma((count,))], 2 * share * n * n,
    )
    update_far = move(update_sent, swapped)
    speaks = jnp.logical_and(stays, col % half == 0) & (lax.axis_index("row") >= 0)
    tip_total = lax.psum(jnp.where(speaks, tip_terms, 0.0), ("tm", "col"))
    fill_block = jnp.where(stays, fill_block, fill_far.astype(F32))
    update = jnp.where(stays, own_update, update_far.astype(F32)) + incoming.astype(F32)
    return (update[None], fill_block[None], tip_block - tip_total)


def solution(mesh):
    return jax.shard_map(
        shards,
        mesh=mesh,
        in_specs=(
            P("tm", ("row", "col"), None),
            P("tm", ("row", "col"), None),
            P("tm", None, ("row", "col"), None),
            P("tm", None, None, None),
            P(),
        ),
        out_specs=(P("tm", ("row", "col"), None), P("tm", ("row", "col"), None), P()),
        check_vma=False,
    )
```

```python
import functools
import jax
import jax.numpy as jnp
from jax import lax
from jax.experimental import pallas as pl
from jax.experimental.pallas import tpu as pltpu
from jax.sharding import PartitionSpec as P

F32, BF16 = jnp.float32, jnp.bfloat16
NT = (((1,), (1,)), ((), ()))
NN = (((1,), (0,)), ((), ()))
AXES = ("tm", "row", "col")
HIGHEST = lax.Precision.HIGHEST


def native(t, c):
    return t % 2 == c // (lax.axis_size("col") // 2)


def move(block, target):
    tms, rows, cols = (lax.axis_size(a) for a in AXES)
    flat = lambda t, r, c: (t * rows + r) * cols + c
    devices = [(t, r, c) for t in range(tms) for r in range(rows) for c in range(cols)]
    route = [(flat(*d), flat(*target(*d))) for d in devices if target(*d) is not None]
    return lax.ppermute(block, AXES, route)


def swapped(t, r, c):
    cols = lax.axis_size("col")
    return (t, r, c) if native(t, c) else (t ^ 1, r, (c + cols // 2) % cols)


def by_row(t, r, c):
    return t, r ^ 1, c


def by_col(t, r, c):
    return t, r, c ^ 1


def by_core(t, r, c):
    return t ^ 1, r, c


def only(keep, target):
    return lambda t, r, c: target(t, r, c) if native(t, c) == keep else None


def swap_or_row(t, r, c):
    return (by_row if native(t, c) else swapped)(t, r, c)


def handed_to(t, r, c):
    half = lax.axis_size("col") // 2
    part = t // 2 * 2 + c // half + 1
    return None if part >= lax.axis_size("tm") else (part, r, c % half + t % 2 * half)


def groups():
    tms, rows, cols = (lax.axis_size(a) for a in AXES)
    half = cols // 2
    return [
        [((2 * x + k) * rows + r) * cols + h * half + c for r in range(rows) for k in range(2) for c in range(half)]
        for x in range(tms // 2)
        for h in range(2)
    ]


def square():
    return lax.axis_size("row") == 2 and lax.axis_size("col") == 4


def begin(both):
    if not square():
        return move(both, swapped), None
    return move(both, swap_or_row), move(both, only(True, by_col))


def spread(both, cut, begun):
    rows, half = lax.axis_size("row"), lax.axis_size("col") // 2
    core = lax.axis_index("tm") % 2
    r, c = lax.axis_index("row"), lax.axis_index("col") % half
    stays = core == lax.axis_index("col") // half
    first, second = begun
    if not square():
        whole = [
            lax.all_gather(x, AXES, axis=0, tiled=False, axis_index_groups=groups())
            for x in (first[:cut], first[cut:])
        ]
        pieces = [[(w[i], 0) for i in range(rows * 2 * half)] for w in whole]
        places = jnp.arange(rows * 2 * half, dtype=jnp.int32)
        yield first
        yield
        yield pieces, jnp.concatenate([places, places])
        return
    gate = yield jnp.where(stays, both, first)
    if gate is not None:
        first, second, _ = lax.optimization_barrier((first, second, gate))
    top_diag = move(jnp.where(stays, second[:cut], first[:cut]), by_row)
    low_diag = move(first[cut:], by_col)
    low_row = move(first[cut:], only(False, by_row))
    top_col = move(first[:cut], only(False, by_col))
    first_core = move(first, by_core)
    gate = yield (top_diag, low_diag, low_row, top_col)
    if gate is not None:
        top_diag, low_diag, low_row, top_col, _ = lax.optimization_barrier(
            (top_diag, low_diag, low_row, top_col, gate)
        )
    top_last = move(top_col, only(False, by_row))
    low_last = move(low_row, only(False, by_col))
    third = jnp.where(stays, both, jnp.concatenate([top_col, low_row], axis=0))
    middle = [top_diag, low_diag, third]
    middle_core = [move(x, by_core) for x in middle]
    fourth = jnp.where(stays, second, jnp.concatenate([top_last, low_last], axis=0))
    mine = [first, *middle, fourth]
    other = [first_core, *middle_core, move(fourth, by_core)]

    def place(k, stays, when, otherwise):
        dr, dc = (jnp.where(stays, a, b) for a, b in zip(when, otherwise))
        return ((r ^ dr) * 2 + k) * half + (c ^ dc)

    moves = ((1, 0), (0, 0)), ((1, 1), (1, 0)), ((1, 1), (0, 1)), ((0, 0), (0, 1)), ((0, 0), (1, 0)), ((0, 1), (1, 1))
    order = (0, 1, 3, 5), (0, 2, 4, 5)
    places = [
        place(k, s, *moves[i]) for o in order for k, s in ((core, stays), (1 - core, ~stays)) for i in o
    ]
    tops = [(x, 0) for side in (mine, other) for x in (side[0], side[1], side[3], side[4])]
    lows = [
        (x, f) for side in (mine, other) for x, f in ((side[0], cut), (side[2], 0), (side[3], cut), (side[4], cut))
    ]
    yield (tops, lows), jnp.stack(places).astype(jnp.int32)


def mm(a, b, dims=NN, precision=None):
    return lax.dot_general(a, b, dims, preferred_element_type=F32, precision=precision)


def split(a):
    hi = a.astype(BF16)
    return hi, (a - hi.astype(F32)).astype(BF16)


def mm3(a, b):
    return mm(a[0], b[0]) + (mm(a[0], b[1]) + mm(a[1], b[0]))


def grid_of(rows, cols, first_row=0, first_col=0):
    row = lax.broadcasted_iota(jnp.int32, (rows, cols), 0) + first_row
    return row, lax.broadcasted_iota(jnp.int32, (rows, cols), 1) + first_col


def copies(firsts, share, places, offset, pieces, whole, sems):
    started = []
    for i, (first, piece) in enumerate(zip(firsts, pieces)):
        at = pl.ds(pl.multiple_of(places[offset + i] * share, 8), share)
        started.append(pltpu.make_async_copy(piece.at[pl.ds(first, share)], whole.at[at], sems.at[i]))
        started[-1].start()
    return started


def wait(started):
    for copy in started:
        copy.wait()


def keep_lower(whole, size):
    n = whole.shape[0]
    for k in range(n // size):
        rows = pl.ds(k * size, size)
        row, col = grid_of(size, n, k * size)
        whole[rows, :] = jnp.where(col <= row, whole[rows, :].astype(F32), 0.0).astype(BF16)


def middle_kernel(size, share, firsts, places, *refs):
    count = len(firsts[0])
    tops, lows = refs[:count], refs[count : 2 * count]
    mid_ref, inverse, rhs, sems = refs[2 * count :]
    one = copies(firsts[0], share, places, 0, tops, inverse, sems.at[0])
    two = copies(firsts[1], share, places, count, lows, rhs, sems.at[1])
    wait(one)
    keep_lower(inverse, size)
    wait(two)
    for k in range(mid_ref.shape[0] // size):
        rows, depth = pl.ds(k * size, size), pl.ds(0, (k + 1) * size)
        mid_ref[:, rows] = mm(rhs[:, depth], inverse[rows, depth], NT).astype(BF16)


def spd_inverse(block, quick):
    size = block.shape[0]
    row, col = grid_of(size, size)
    eye = (row == col).astype(F32)
    start = eye / jnp.sum(jnp.abs(block), axis=0, keepdims=True)
    parts = split(block)
    guess = start
    for _ in range(quick):
        short = guess.astype(BF16)
        guess = 2.0 * guess - mm(short, mm(parts[0], short).astype(BF16))

    def gap_of(x):
        gap = eye - mm3(parts, split(x))
        return gap, jnp.max(jnp.sum(jnp.abs(gap), axis=0, keepdims=True))

    _, worst = gap_of(guess)
    good = worst < 0.5
    guess = jnp.where(good, guess, start)

    def go(state):
        turn, worst, _ = state
        return jnp.logical_and(turn < 60, worst > 2e-2)

    def step(state):
        turn, _, x = state
        gap, _ = gap_of(x)
        x = x + mm3(split(x), split(gap))
        return turn + 1, gap_of(x)[1], x

    guess = lax.while_loop(go, step, (0, jnp.where(good, worst, 1.0), guess))[2]
    return guess + mm3(split(guess), split(gap_of(guess)[0]))


def factor_kernel(size, quick, share, firsts, places, mid, diag, *refs):
    count = len(firsts)
    tops = refs[:count]
    low_ref, inv_ref, packed, block, sems = refs[count:]
    started = copies(firsts, share, places, 0, tops, packed, sems)
    blocks = mid.shape[0] // size
    at = lambda k: pl.ds(k * size, size)
    wait(started)
    for k in range(blocks):
        for j in range(k, blocks):
            own = packed[at(k), at(j)].astype(F32)
            if j == k:
                row, col = grid_of(size, size)
                own = jnp.where(col > row, own, 0.0)
                own = own + own.T + jnp.where(col == row, diag[:, at(k)], 0.0)
            else:
                own = own.T
            block[at(j), at(k)] = own - mm(mid[at(j), :], mid[at(k), :], NT)
    for k in range(blocks):
        inverse = spd_inverse(block[at(k), at(k)], quick).astype(BF16)
        inv_ref[at(k), :] = inverse
        for j in range(k + 1, blocks):
            low_ref[at(j), at(k)] = mm(block[at(j), at(k)].astype(BF16), inverse).astype(BF16)
        for j in range(k + 1, blocks):
            low = low_ref[at(j), at(k)]
            for i in range(j, blocks):
                block[at(i), at(j)] -= mm(block[at(i), at(k)].astype(BF16), low, NT)


def solve_kernel(size, share, firsts, places, mid, low_ref, inv, own_top, own_low, arrows, *refs):
    count = len(firsts)
    tops = refs[:count]
    upper_ref, left_ref, tip_ref, inverse, top, rows, solved, sems = refs[count:]
    started = copies(firsts, share, places, 0, tops, inverse, sems)
    n = mid.shape[0]
    blocks, fixed = n // size, arrows.shape[0] // 2
    at = lambda k: pl.ds(k * size, size)
    wait(started)
    keep_lower(inverse, size)
    terms, rest = [], arrows[:fixed]
    for _ in range(3):
        terms.append(rest.astype(BF16).astype(F32))
        rest = rest - terms[-1]
    thin = jnp.concatenate(terms, axis=0).astype(BF16)
    arrow_parts = mm(thin, inverse[...], NT)
    arrow_one = arrow_parts[:fixed] + arrow_parts[fixed : 2 * fixed] + arrow_parts[2 * fixed :]
    for k in range(blocks):
        depth = pl.ds(0, (k + 1) * size)
        top[:, at(k)] = mm(own_top[:, depth], inverse[at(k), depth], NT).astype(BF16)
    rows[:share] = -mm(top[...], mid[...], NT)
    rows[share : 2 * share] = own_low[...].astype(F32)
    arrow_two = arrows[fixed:] - mm(arrow_one.astype(BF16), mid[...], NT)
    rows[2 * share :] = arrow_two
    for k in range(blocks):
        row = rows[:, at(k)].astype(BF16)
        solved[:, at(k)] = mm(row, inv[at(k), :])
        if k + 1 < blocks:
            rest = pl.ds((k + 1) * size, n - (k + 1) * size)
            rows[:, rest] -= mm(row, low_ref[rest, at(k)], NT)
    for k in range(blocks - 2, -1, -1):
        rest = pl.ds((k + 1) * size, n - (k + 1) * size)
        solved[:, at(k)] -= mm(solved[:, rest].astype(BF16), low_ref[rest, at(k)])
    upper_ref[...] = solved[: 2 * share].astype(BF16)
    left = (top[...].astype(F32) - mm(upper_ref[:share], mid[...])).astype(BF16)
    for k in range(blocks):
        depth = pl.ds(k * size, n - k * size)
        left_ref[:, at(k)] = mm(left[:, k * size :], inverse[depth, at(k)]).astype(BF16)
    tip_ref[...] = mm(arrow_one, arrow_one, NT, HIGHEST) + mm(solved[2 * share :], arrow_two, NT, HIGHEST)


def product_kernel(share, firsts, offset, signs, places, left, *refs):
    count = len(firsts)
    pieces = refs[:count]
    outs, (whole, sems) = refs[count:-2], refs[-2:]
    started = copies(firsts, share, places, offset, pieces, whole, sems)
    wait(started)
    for i, sign in enumerate(signs):
        product = mm(left[i * share : (i + 1) * share], whole[...], NT)
        product = product if sign > 0 else -product
        outs[2 * i][...] = product
        outs[2 * i + 1][...] = product.astype(BF16)


VMEM = pl.BlockSpec(memory_space=pltpu.VMEM)
ANY = pl.BlockSpec(memory_space=pl.ANY)
SMEM = pl.BlockSpec(memory_space=pltpu.SMEM)


def call(kernel, name, outs, places, dense, pieces, scratch, flops):
    arrays = [array for array, _ in pieces]
    size = lambda x: x.size * x.dtype.itemsize
    return pl.pallas_call(
        kernel,
        out_shape=outs,
        in_specs=[SMEM] + [VMEM] * len(dense) + [ANY] * len(arrays),
        out_specs=[VMEM] * len(outs),
        scratch_shapes=scratch,
        compiler_params=pltpu.CompilerParams(vmem_limit_bytes=36 << 20),
        cost_estimate=pl.CostEstimate(
            flops=flops, bytes_accessed=sum(map(size, [*dense, *arrays, *outs])), transcendentals=0
        ),
        name=name,
    )(places, *dense, *arrays)


def shards(first_inverse, second_diag, coupling, arrow_rows, tip_block):
    share, n = coupling.shape[2:]
    size = 256 if n % 256 == 0 else 128
    cols = lax.axis_size("col")
    half, fixed = cols // 2, arrow_rows.shape[2]
    core, col = lax.axis_index("tm") % 2, lax.axis_index("col")
    stays = core == col // half
    shape = jax.ShapeDtypeStruct
    dma = pltpu.SemaphoreType.DMA

    row, column = grid_of(share, n, (lax.axis_index("row") * cols + col) * share)
    diag_own = jnp.sum(jnp.where(row == column, second_diag[0], 0), axis=0, keepdims=True)
    packed = jnp.where(column <= row, first_inverse[0], second_diag[0])
    packed = jnp.concatenate([packed, jnp.pad(diag_own, ((0, 15), (0, 0)))], axis=0)
    arrows = move(arrow_rows[0].reshape(2 * fixed, n), swapped)
    both = jnp.concatenate([packed, coupling[0, 1]], axis=0)
    cut = packed.shape[0]
    one = spread(both, cut, begin(both))
    next(one)
    gate = one.send(None)
    both = jnp.concatenate([coupling[0, 2], coupling[0, 0]], axis=0)
    if gate is not None:
        both, _ = lax.optimization_barrier((both, gate))
    two = spread(both, share, begin(both))
    own = next(two)
    (tops, lows), places = one.send(None)
    own_low, own_top = own[:share], own[share:]
    diag = sum(array[share : share + 1].astype(F32) for array, _ in tops)

    firsts = [[f for _, f in p] for p in (tops, lows)]
    count = len(tops)
    whole = pltpu.VMEM((n, n), BF16)
    (mid,) = call(
        functools.partial(middle_kernel, size, share, firsts), "middle",
        [shape((n, n), BF16)], places, [], tops + lows, [whole, whole, dma((2, count))], n**3,
    )
    two.send(mid)
    low, inverses = call(
        functools.partial(factor_kernel, size, 4, share, firsts[0]), "factor",
        [shape((n, n), BF16), shape((n, size), BF16)], places, [mid, diag], tops,
        [whole, pltpu.VMEM((n, n), F32), dma((count,))], 2 * n**3,
    )
    (low_pieces, top_pieces), later = two.send(inverses)
    solved, left, tip_terms = call(
        functools.partial(solve_kernel, size, share, firsts[0]), "solve",
        [shape((2 * share, n), BF16), shape((share, n), BF16), shape((fixed, fixed), F32)],
        places, [mid, low, inverses, own_top, own_low, arrows], tops,
        [whole, pltpu.VMEM((share, n), BF16), pltpu.VMEM((2 * share + fixed, n), F32),
         pltpu.VMEM((2 * share + fixed, n), F32), dma((count,))], 8 * share * n * n,
    )
    out = [shape((share, n), F32), shape((share, n), BF16)]
    firsts = [[f for _, f in p] for p in (low_pieces, top_pieces)]
    fill_block, fill_sent, _, handed = call(
        functools.partial(product_kernel, share, firsts[0], 0, (-1, 1)), "fill",
        out + out, later, [solved], low_pieces, [whole, dma((count,))], 4 * share * n * n,
    )
    incoming = move(handed, handed_to)
    fill_far = move(fill_sent, swapped)
    own_update, update_sent = call(
        functools.partial(product_kernel, share, firsts[1], count, (1,)), "update",
        out, later, [left], top_pieces, [whole, dma((count,))], 2 * share * n * n,
    )
    update_far = move(update_sent, swapped)
    tip_total = lax.psum(move(tip_terms, swapped), "tm")
    fill_block = jnp.where(stays, fill_block, fill_far.astype(F32))
    update = jnp.where(stays, own_update, update_far.astype(F32)) + incoming.astype(F32)
    return (update[None], fill_block[None], tip_block - tip_total)


def solution(mesh):
    return jax.shard_map(
        shards,
        mesh=mesh,
        in_specs=(
            P("tm", ("row", "col"), None),
            P("tm", ("row", "col"), None),
            P("tm", None, ("row", "col"), None),
            P("tm", None, None, None),
            P(),
        ),
        out_specs=(P("tm", ("row", "col"), None), P("tm", ("row", "col"), None), P()),
        check_vma=False,
    )
```

```python
import functools
import jax
import jax.numpy as jnp
from jax import lax
from jax.experimental import pallas as pl
from jax.experimental.pallas import tpu as pltpu
from jax.sharding import PartitionSpec as P

F32, BF16 = jnp.float32, jnp.bfloat16
NT = (((1,), (1,)), ((), ()))
NN = (((1,), (0,)), ((), ()))
AXES = ("tm", "row", "col")
HIGHEST = lax.Precision.HIGHEST


def native(t, c):
    return t % 2 == c // (lax.axis_size("col") // 2)


def move(block, target):
    tms, rows, cols = (lax.axis_size(a) for a in AXES)
    flat = lambda t, r, c: (t * rows + r) * cols + c
    devices = [(t, r, c) for t in range(tms) for r in range(rows) for c in range(cols)]
    route = [(flat(*d), flat(*target(*d))) for d in devices if target(*d) is not None]
    return lax.ppermute(block, AXES, route)


def swapped(t, r, c):
    cols = lax.axis_size("col")
    return (t, r, c) if native(t, c) else (t ^ 1, r, (c + cols // 2) % cols)


def by_row(t, r, c):
    return t, r ^ 1, c


def by_col(t, r, c):
    return t, r, c ^ 1


def by_core(t, r, c):
    return t ^ 1, r, c


def only(keep, target):
    return lambda t, r, c: target(t, r, c) if native(t, c) == keep else None


def swap_or_row(t, r, c):
    return (by_row if native(t, c) else swapped)(t, r, c)


def handed_to(t, r, c):
    half = lax.axis_size("col") // 2
    part = t // 2 * 2 + c // half + 1
    return None if part >= lax.axis_size("tm") else (part, r, c % half + t % 2 * half)


def groups():
    tms, rows, cols = (lax.axis_size(a) for a in AXES)
    half = cols // 2
    return [
        [((2 * x + k) * rows + r) * cols + h * half + c for r in range(rows) for k in range(2) for c in range(half)]
        for x in range(tms // 2)
        for h in range(2)
    ]


def square():
    return lax.axis_size("row") == 2 and lax.axis_size("col") == 4


def begin(both):
    if not square():
        return move(both, swapped), None
    return move(both, swap_or_row), move(both, only(True, by_col))


def spread(both, cut, begun):
    rows, half = lax.axis_size("row"), lax.axis_size("col") // 2
    core = lax.axis_index("tm") % 2
    r, c = lax.axis_index("row"), lax.axis_index("col") % half
    stays = core == lax.axis_index("col") // half
    first, second = begun
    if not square():
        whole = [
            lax.all_gather(x, AXES, axis=0, tiled=False, axis_index_groups=groups())
            for x in (first[:cut], first[cut:])
        ]
        pieces = [[(w[i], 0) for i in range(rows * 2 * half)] for w in whole]
        places = jnp.arange(rows * 2 * half, dtype=jnp.int32)
        gate = yield first
        gate = yield gate, None
        gate = yield gate
        yield gate, pieces, jnp.concatenate([places, places])
        return
    gate = yield jnp.where(stays, both, first)
    first, second, gate = lax.optimization_barrier((first, second, gate))
    top_diag = move(jnp.where(stays, second[:cut], first[:cut]), by_row)
    low_diag = move(first[cut:], by_col)
    low_row = move(first[cut:], only(False, by_row))
    top_col = move(first[:cut], only(False, by_col))
    first_core = move(first, by_core)
    sent = yield gate, (top_diag, low_diag, low_row, top_col)
    top_diag, low_diag, low_row, top_col, gate = lax.optimization_barrier(
        (top_diag, low_diag, low_row, top_col, sent)
    )
    top_last = move(top_col, only(False, by_row))
    low_last = move(low_row, only(False, by_col))
    third = jnp.where(stays, both, jnp.concatenate([top_col, low_row], axis=0))
    middle = [top_diag, low_diag, third]
    middle_core = [move(x, by_core) for x in middle]
    sent = yield gate
    top_last, low_last, second, gate = lax.optimization_barrier((top_last, low_last, second, sent))
    fourth = jnp.where(stays, second, jnp.concatenate([top_last, low_last], axis=0))
    mine = [first, *middle, fourth]
    other = [first_core, *middle_core, move(fourth, by_core)]

    def place(k, stays, when, otherwise):
        dr, dc = (jnp.where(stays, a, b) for a, b in zip(when, otherwise))
        return ((r ^ dr) * 2 + k) * half + (c ^ dc)

    moves = ((1, 0), (0, 0)), ((1, 1), (1, 0)), ((1, 1), (0, 1)), ((0, 0), (0, 1)), ((0, 0), (1, 0)), ((0, 1), (1, 1))
    order = (0, 1, 3, 5), (0, 2, 4, 5)
    places = [
        place(k, s, *moves[i]) for o in order for k, s in ((core, stays), (1 - core, ~stays)) for i in o
    ]
    tops = [(x, 0) for side in (mine, other) for x in (side[0], side[1], side[3], side[4])]
    lows = [
        (x, f) for side in (mine, other) for x, f in ((side[0], cut), (side[2], 0), (side[3], cut), (side[4], cut))
    ]
    yield gate, (tops, lows), jnp.stack(places).astype(jnp.int32)


def mm(a, b, dims=NN, precision=None):
    return lax.dot_general(a, b, dims, preferred_element_type=F32, precision=precision)


def split(a):
    hi = a.astype(BF16)
    return hi, (a - hi.astype(F32)).astype(BF16)


def mm3(a, b):
    return mm(a[0], b[0]) + (mm(a[0], b[1]) + mm(a[1], b[0]))


def grid_of(rows, cols, first_row=0, first_col=0):
    row = lax.broadcasted_iota(jnp.int32, (rows, cols), 0) + first_row
    return row, lax.broadcasted_iota(jnp.int32, (rows, cols), 1) + first_col


def copies(firsts, share, places, offset, pieces, whole, sems):
    started = []
    for i, (first, piece) in enumerate(zip(firsts, pieces)):
        at = pl.ds(pl.multiple_of(places[offset + i] * share, 8), share)
        started.append(pltpu.make_async_copy(piece.at[pl.ds(first, share)], whole.at[at], sems.at[i]))
        started[-1].start()
    return started


def wait(started):
    for copy in started:
        copy.wait()


def middle_kernel(size, share, firsts, places, *refs):
    count = len(firsts[0])
    tops, lows = refs[:count], refs[count : 2 * count]
    mid_ref, packed, inverse, token, rhs, sems = refs[2 * count :]
    one = copies(firsts[0], share, places, 0, tops, packed, sems.at[0])
    two = copies(firsts[1], share, places, count, lows, rhs, sems.at[1])
    n = mid_ref.shape[0]
    at = lambda k: pl.ds(k * size, size)
    token[...] = jnp.zeros_like(token)
    wait(one)
    for k in range(n // size):
        row, col = grid_of(size, n, k * size)
        inverse[at(k), :] = jnp.where(col <= row, packed[at(k), :].astype(F32), 0.0).astype(BF16)
    wait(two)
    for k in range(n // size):
        depth = pl.ds(0, (k + 1) * size)
        mid_ref[:, at(k)] = mm(rhs[:, depth], inverse[at(k), depth], NT).astype(BF16)


def spd_inverse(block, quick):
    size = block.shape[0]
    row, col = grid_of(size, size)
    eye = (row == col).astype(F32)
    across = 1.0 / jnp.sum(jnp.abs(block), axis=0, keepdims=True)
    down = 1.0 / jnp.sum(jnp.abs(block), axis=1, keepdims=True)
    start = eye * (2.0 * across) - down * block * across
    parts = split(block)
    guess = start
    for _ in range(quick):
        short = guess.astype(BF16)
        guess = 2.0 * guess - mm(short, mm(parts[0], short).astype(BF16))

    def state_of(turn, x):
        gap = eye - mm3(parts, split(x))
        return turn, jnp.max(jnp.sum(jnp.abs(gap), axis=0, keepdims=True)), x, gap

    def better(state):
        return state[2] + mm3(split(state[2]), split(state[3]))

    state = state_of(0, guess)
    state = lax.cond(state[1] < 0.5, lambda: state, lambda: state_of(0, start))
    state = lax.while_loop(
        lambda state: jnp.logical_and(state[0] < 60, state[1] > 2e-2),
        lambda state: state_of(state[0] + 1, better(state)),
        state,
    )
    return better(state)


def eliminate(size, quick, tile, low_ref, inv_ref, low_row, first, cut, blocks):
    at = lambda k: pl.ds(k * size, size)
    for k in range(first, cut):
        inverse = spd_inverse(tile(k, k)[...], quick).astype(BF16)
        inv_ref[at(k - first), :] = inverse
        for j in range(k + 1, blocks):
            low_ref[at(j - low_row), at(k - first)] = mm(tile(j, k)[...].astype(BF16), inverse).astype(BF16)
        for j in range(k + 1, blocks):
            low = low_ref[at(j - low_row), at(k - first)]
            for i in range(j, blocks):
                tile(i, j)[...] -= mm(tile(i, k)[...].astype(BF16), low, NT)


def factor_kernel(size, quick, _, __, mid, packed, diag, low_ref, inv_ref, rest, token, block):
    blocks = mid.shape[0] // size
    cut = blocks // 2
    at = lambda k: pl.ds(k * size, size)

    def tile(i, j):
        return rest.at[at(i - cut), at(j - cut)] if j >= cut else block.at[at(i), at(j)]

    token[...] = jnp.zeros_like(token)
    for k in range(blocks):
        for j in range(k, blocks):
            own = packed[at(k), at(j)].astype(F32)
            if j == k:
                row, col = grid_of(size, size)
                own = jnp.where(col > row, own, 0.0)
                own = own + own.T + jnp.where(col == row, diag[:, at(k)], 0.0)
            else:
                own = own.T
            tile(j, k)[...] = own - mm(mid[at(j), :], mid[at(k), :], NT)
    eliminate(size, quick, tile, low_ref, inv_ref, 0, 0, cut, blocks)


def finish_kernel(size, quick, _, __, rest, low_ref, inv_ref, token, block):
    at = lambda k: pl.ds(k * size, size)
    token[...] = jnp.zeros_like(token)
    block[...] = rest[...]
    blocks = rest.shape[0] // size
    eliminate(size, quick, lambda i, j: block.at[at(i), at(j)], low_ref, inv_ref, 0, 0, blocks, blocks)


def solve_kernel(size, share, _, __, mid, inverse, low_one, inv_one, low_two, inv_two, own_top, own_low, arrows, *refs):
    upper_ref, left_ref, tip_ref, top, rows, solved = refs
    n = mid.shape[0]
    blocks, fixed = n // size, arrows.shape[0] // 2
    cut = blocks // 2
    at = lambda k: pl.ds(k * size, size)

    def low(k):
        if k < cut:
            return low_one[pl.ds((k + 1) * size, n - (k + 1) * size), at(k)]
        return low_two[pl.ds((k + 1 - cut) * size, n - (k + 1) * size), at(k - cut)]

    terms, rest = [], arrows[:fixed]
    for _ in range(3):
        terms.append(rest.astype(BF16).astype(F32))
        rest = rest - terms[-1]
    thin = jnp.concatenate(terms, axis=0).astype(BF16)
    arrow_parts = mm(thin, inverse[...], NT)
    arrow_one = arrow_parts[:fixed] + arrow_parts[fixed : 2 * fixed] + arrow_parts[2 * fixed :]
    for k in range(blocks):
        depth = pl.ds(0, (k + 1) * size)
        top[:, at(k)] = mm(own_top[:, depth], inverse[at(k), depth], NT).astype(BF16)
    rows[:share] = -mm(top[...], mid[...], NT)
    rows[share : 2 * share] = own_low[...].astype(F32)
    arrow_two = arrows[fixed:] - mm(arrow_one.astype(BF16), mid[...], NT)
    rows[2 * share :] = arrow_two
    for k in range(blocks):
        row = rows[:, at(k)].astype(BF16)
        solved[:, at(k)] = mm(row, inv_one[at(k), :] if k < cut else inv_two[at(k - cut), :])
        if k + 1 < blocks:
            rows[:, pl.ds((k + 1) * size, n - (k + 1) * size)] -= mm(row, low(k), NT)
    for k in range(blocks - 2, -1, -1):
        after = solved[:, pl.ds((k + 1) * size, n - (k + 1) * size)]
        solved[:, at(k)] -= mm(after.astype(BF16), low(k))
    upper_ref[...] = solved[: 2 * share].astype(BF16)
    left = (top[...].astype(F32) - mm(upper_ref[:share], mid[...])).astype(BF16)
    for k in range(blocks):
        depth = pl.ds(k * size, n - k * size)
        left_ref[:, at(k)] = mm(left[:, k * size :], inverse[depth, at(k)]).astype(BF16)
    tip_ref[...] = mm(arrow_one, arrow_one, NT, HIGHEST) + mm(solved[2 * share :], arrow_two, NT, HIGHEST)


def product_kernel(share, firsts, offset, signs, places, left, *refs):
    count = len(firsts)
    pieces = refs[:count]
    outs, (whole, sems) = refs[count:-2], refs[-2:]
    started = copies(firsts, share, places, offset, pieces, whole, sems)
    wait(started)
    for i, sign in enumerate(signs):
        product = mm(left[i * share : (i + 1) * share], whole[...], NT)
        product = product if sign > 0 else -product
        outs[2 * i][...] = product
        outs[2 * i + 1][...] = product.astype(BF16)


VMEM = pl.BlockSpec(memory_space=pltpu.VMEM)
ANY = pl.BlockSpec(memory_space=pl.ANY)
SMEM = pl.BlockSpec(memory_space=pltpu.SMEM)


def call(kernel, name, outs, places, dense, pieces, scratch, flops):
    arrays = [array for array, _ in pieces]
    size = lambda x: x.size * x.dtype.itemsize
    return pl.pallas_call(
        kernel,
        out_shape=outs,
        in_specs=[SMEM] + [VMEM] * len(dense) + [ANY] * len(arrays),
        out_specs=[VMEM] * len(outs),
        scratch_shapes=scratch,
        compiler_params=pltpu.CompilerParams(vmem_limit_bytes=26 << 20),
        cost_estimate=pl.CostEstimate(
            flops=flops, bytes_accessed=sum(map(size, [*dense, *arrays, *outs])), transcendentals=0
        ),
        name=name,
    )(places, *dense, *arrays)


def shards(first_inverse, second_diag, coupling, arrow_rows, tip_block):
    share, n = coupling.shape[2:]
    size = 256 if n % 256 == 0 else 128
    cols = lax.axis_size("col")
    half, fixed = cols // 2, arrow_rows.shape[2]
    core, col = lax.axis_index("tm") % 2, lax.axis_index("col")
    stays = core == col // half
    shape = jax.ShapeDtypeStruct
    dma = pltpu.SemaphoreType.DMA

    row, column = grid_of(share, n, (lax.axis_index("row") * cols + col) * share)
    diag_own = jnp.sum(jnp.where(row == column, second_diag[0], 0), axis=0, keepdims=True)
    packed = jnp.where(column <= row, first_inverse[0], second_diag[0])
    packed = jnp.concatenate([packed, jnp.pad(diag_own, ((0, 15), (0, 0)))], axis=0)
    arrows = move(arrow_rows[0].reshape(2 * fixed, n), swapped)
    both = jnp.concatenate([packed, coupling[0, 1]], axis=0)
    cut = packed.shape[0]
    one = spread(both, cut, begin(both))
    next(one)
    _, gate = one.send(())
    both = jnp.concatenate([coupling[0, 2], coupling[0, 0]], axis=0)
    if gate is not None:
        both, _ = lax.optimization_barrier((both, gate))
    two = spread(both, share, begin(both))
    own = next(two)
    one.send(())
    _, (tops, lows), places = one.send(())
    own_low, own_top = own[:share], own[share:]
    diag = sum(array[share : share + 1].astype(F32) for array, _ in tops)

    firsts = [[f for _, f in p] for p in (tops, lows)]
    count = len(tops)
    whole = pltpu.VMEM((n, n), BF16)
    square_shape, token_shape = shape((n, n), BF16), shape((8, 128), F32)
    mid, packed, inverse, token = call(
        functools.partial(middle_kernel, size, share, firsts), "middle",
        [square_shape] * 3 + [token_shape], places, [], tops + lows, [whole, dma((2, count))], n**3,
    )
    (token, arrows), _ = two.send((token, arrows))
    cut = n // size // 2 * size
    rest = n - cut
    low_one, inv_one, block, token = call(
        functools.partial(factor_kernel, size, 3), "factor",
        [shape((n, cut), BF16), shape((cut, size), BF16), shape((rest, rest), F32), token_shape],
        places, [token, mid, packed, diag], [], [pltpu.VMEM((n, cut), F32)], 2 * n**3,
    )
    token = two.send(token)
    low_two, inv_two, token = call(
        functools.partial(finish_kernel, size, 3), "finish",
        [shape((rest, rest), BF16), shape((rest, size), BF16), token_shape],
        places, [token, block], [], [pltpu.VMEM((rest, rest), F32)], rest**3,
    )
    token, (low_pieces, top_pieces), later = two.send(token)
    solved, left, tip_terms = call(
        functools.partial(solve_kernel, size, share), "solve",
        [shape((2 * share, n), BF16), shape((share, n), BF16), shape((fixed, fixed), F32)],
        places, [token, mid, inverse, low_one, inv_one, low_two, inv_two, own_top, own_low, arrows], [],
        [pltpu.VMEM((share, n), BF16)] + [pltpu.VMEM((2 * share + fixed, n), F32)] * 2, 8 * share * n * n,
    )
    out = [shape((share, n), F32), shape((share, n), BF16)]
    firsts = [[f for _, f in p] for p in (low_pieces, top_pieces)]
    fill_block, fill_sent, _, handed = call(
        functools.partial(product_kernel, share, firsts[0], 0, (-1, 1)), "fill",
        out + out, later, [solved], low_pieces, [whole, dma((count,))], 4 * share * n * n,
    )
    incoming = move(handed, handed_to)
    fill_far = move(fill_sent, swapped)
    own_update, update_sent = call(
        functools.partial(product_kernel, share, firsts[1], count, (1,)), "update",
        out, later, [left], top_pieces, [whole, dma((count,))], 2 * share * n * n,
    )
    update_far = move(update_sent, swapped)
    tip_total = move(tip_terms, swapped)
    if lax.axis_size("tm") == 4:
        for bit in (1, 2):
            tip_total += move(tip_total, lambda t, r, c: (t ^ bit, r, c))
    else:
        tip_total = lax.psum(tip_total, "tm")
    fill_block = jnp.where(stays, fill_block, fill_far.astype(F32))
    update = jnp.where(stays, own_update, update_far.astype(F32)) + incoming.astype(F32)
    return (update[None], fill_block[None], tip_block - tip_total)


def solution(mesh):
    return jax.shard_map(
        shards,
        mesh=mesh,
        in_specs=(
            P("tm", ("row", "col"), None),
            P("tm", ("row", "col"), None),
            P("tm", None, ("row", "col"), None),
            P("tm", None, None, None),
            P(),
        ),
        out_specs=(P("tm", ("row", "col"), None), P("tm", ("row", "col"), None), P()),
        check_vma=False,
    )
```

```python
import functools
import jax
import jax.numpy as jnp
from jax import lax
from jax.experimental import pallas as pl
from jax.experimental.pallas import tpu as pltpu
from jax.sharding import PartitionSpec as P


F32, BF16 = jnp.float32, jnp.bfloat16
NT = (((1,), (1,)), ((), ()))
NN = (((1,), (0,)), ((), ()))
AXES = ("tm", "row", "col")
HIGHEST = lax.Precision.HIGHEST


def native(t, c):
    return t % 2 == c // (lax.axis_size("col") // 2)


def move(block, target):
    tms, rows, cols = (lax.axis_size(a) for a in AXES)
    flat = lambda t, r, c: (t * rows + r) * cols + c
    devices = [(t, r, c) for t in range(tms) for r in range(rows) for c in range(cols)]
    route = [(flat(*d), flat(*target(*d))) for d in devices if target(*d) is not None]
    return lax.ppermute(block, AXES, route)


def swapped(t, r, c):
    cols = lax.axis_size("col")
    return (t, r, c) if native(t, c) else (t ^ 1, r, (c + cols // 2) % cols)


def by_row(t, r, c):
    return t, r ^ 1, c


def by_col(t, r, c):
    return t, r, c ^ 1


def by_core(t, r, c):
    return t ^ 1, r, c


def only(keep, target):
    return lambda t, r, c: target(t, r, c) if native(t, c) == keep else None


def swap_or_row(t, r, c):
    return (by_row if native(t, c) else swapped)(t, r, c)


def handed_to(t, r, c):
    half = lax.axis_size("col") // 2
    part = t // 2 * 2 + c // half + 1
    return None if part >= lax.axis_size("tm") else (part, r, c % half + t % 2 * half)


def groups():
    tms, rows, cols = (lax.axis_size(a) for a in AXES)
    half = cols // 2
    return [
        [((2 * x + k) * rows + r) * cols + h * half + c for r in range(rows) for k in range(2) for c in range(half)]
        for x in range(tms // 2)
        for h in range(2)
    ]


def square():
    return lax.axis_size("row") == 2 and lax.axis_size("col") == 4


def begin(both):
    if not square():
        return move(both, swapped), None
    return move(both, swap_or_row), move(both, only(True, by_col))


def spread(both, cut, begun):
    rows, half = lax.axis_size("row"), lax.axis_size("col") // 2
    core = lax.axis_index("tm") % 2
    r, c = lax.axis_index("row"), lax.axis_index("col") % half
    stays = core == lax.axis_index("col") // half
    first, second = begun
    if not square():
        whole = [
            lax.all_gather(x, AXES, axis=0, tiled=False, axis_index_groups=groups())
            for x in (first[:cut], first[cut:])
        ]
        pieces = [[(w[i], 0) for i in range(rows * 2 * half)] for w in whole]
        places = jnp.arange(rows * 2 * half, dtype=jnp.int32)
        gate = yield first
        gate = yield gate, None
        gate = yield gate
        yield gate, pieces, jnp.concatenate([places, places])
        return
    gate = yield jnp.where(stays, both, first)
    first, second, gate = lax.optimization_barrier((first, second, gate))
    top_diag = move(jnp.where(stays, second[:cut], first[:cut]), by_row)
    low_diag = move(first[cut:], by_col)
    low_row = move(first[cut:], only(False, by_row))
    top_col = move(first[:cut], only(False, by_col))
    first_core = move(first, by_core)
    sent = yield gate, (top_diag, low_diag, low_row, top_col)
    top_diag, low_diag, low_row, top_col, gate = lax.optimization_barrier(
        (top_diag, low_diag, low_row, top_col, sent)
    )
    top_last = move(top_col, only(False, by_row))
    low_last = move(low_row, only(False, by_col))
    third = jnp.where(stays, both, jnp.concatenate([top_col, low_row], axis=0))
    middle = [top_diag, low_diag, third]
    middle_core = [move(x, by_core) for x in middle]
    sent = yield gate
    top_last, low_last, second, gate = lax.optimization_barrier((top_last, low_last, second, sent))
    fourth = jnp.where(stays, second, jnp.concatenate([top_last, low_last], axis=0))
    mine = [first, *middle, fourth]
    other = [first_core, *middle_core, move(fourth, by_core)]

    def place(k, stays, when, otherwise):
        dr, dc = (jnp.where(stays, a, b) for a, b in zip(when, otherwise))
        return ((r ^ dr) * 2 + k) * half + (c ^ dc)

    moves = ((1, 0), (0, 0)), ((1, 1), (1, 0)), ((1, 1), (0, 1)), ((0, 0), (0, 1)), ((0, 0), (1, 0)), ((0, 1), (1, 1))
    order = (0, 1, 3, 5), (0, 2, 4, 5)
    places = [
        place(k, s, *moves[i]) for o in order for k, s in ((core, stays), (1 - core, ~stays)) for i in o
    ]
    tops = [(x, 0) for side in (mine, other) for x in (side[0], side[1], side[3], side[4])]
    lows = [
        (x, f) for side in (mine, other) for x, f in ((side[0], cut), (side[2], 0), (side[3], cut), (side[4], cut))
    ]
    yield gate, (tops, lows), jnp.stack(places).astype(jnp.int32)


def mm(a, b, dims=NN, precision=None):
    return lax.dot_general(a, b, dims, preferred_element_type=F32, precision=precision)


def split(a):
    hi = a.astype(BF16)
    return hi, (a - hi.astype(F32)).astype(BF16)


def mm3(a, b):
    return mm(a[0], b[0]) + (mm(a[0], b[1]) + mm(a[1], b[0]))


def grid_of(rows, cols, first_row=0, first_col=0):
    row = lax.broadcasted_iota(jnp.int32, (rows, cols), 0) + first_row
    return row, lax.broadcasted_iota(jnp.int32, (rows, cols), 1) + first_col


def copies(firsts, share, places, offset, pieces, whole, sems):
    started = []
    for i, (first, piece) in enumerate(zip(firsts, pieces)):
        at = pl.ds(pl.multiple_of(places[offset + i] * share, 8), share)
        started.append(pltpu.make_async_copy(piece.at[pl.ds(first, share)], whole.at[at], sems.at[i]))
        started[-1].start()
    return started


def wait(started):
    for copy in started:
        copy.wait()


def middle_kernel(size, share, firsts, places, *refs):
    count = len(firsts[0])
    tops, lows = refs[:count], refs[count : 2 * count]
    mid_ref, packed, inverse, token, rhs, sems = refs[2 * count :]
    one = copies(firsts[0], share, places, 0, tops, packed, sems.at[0])
    two = copies(firsts[1], share, places, count, lows, rhs, sems.at[1])
    n = mid_ref.shape[0]
    at = lambda k: pl.ds(k * size, size)
    token[...] = jnp.zeros_like(token)
    wait(one)
    for k in range(n // size):
        row, col = grid_of(size, n, k * size)
        inverse[at(k), :] = jnp.where(col <= row, packed[at(k), :].astype(F32), 0.0).astype(BF16)
    wait(two)
    for k in range(n // size):
        depth = pl.ds(0, (k + 1) * size)
        mid_ref[:, at(k)] = mm(rhs[:, depth], inverse[at(k), depth], NT).astype(BF16)


def spd_inverse(block, quick):
    size = block.shape[0]
    row, col = grid_of(size, size)
    eye = (row == col).astype(F32)
    across = 1.0 / jnp.sum(jnp.abs(block), axis=0, keepdims=True)
    down = 1.0 / jnp.sum(jnp.abs(block), axis=1, keepdims=True)
    start = eye * (2.0 * across) - down * block * across
    parts = split(block)
    guess = start
    for _ in range(quick):
        short = guess.astype(BF16)
        guess = 2.0 * guess - mm(short, mm(parts[0], short).astype(BF16))

    def state_of(turn, x):
        gap = eye - mm3(parts, split(x))
        return turn, jnp.max(jnp.sum(jnp.abs(gap), axis=0, keepdims=True)), x, gap

    def better(state):
        return state[2] + mm3(split(state[2]), split(state[3]))

    state = state_of(0, guess)
    state = lax.cond(state[1] < 0.5, lambda: state, lambda: state_of(0, start))
    state = lax.while_loop(
        lambda state: jnp.logical_and(state[0] < 60, state[1] > 2e-2),
        lambda state: state_of(state[0] + 1, better(state)),
        state,
    )
    return better(state)


def eliminate(size, quick, tile, low_ref, inv_ref, low_row, first, cut, blocks):
    at = lambda k: pl.ds(k * size, size)
    for k in range(first, cut):
        inverse = spd_inverse(tile(k, k)[...], quick).astype(BF16)
        inv_ref[at(k - first), :] = inverse
        for j in range(k + 1, blocks):
            low_ref[at(j - low_row), at(k - first)] = mm(tile(j, k)[...].astype(BF16), inverse).astype(BF16)
        for j in range(k + 1, blocks):
            low = low_ref[at(j - low_row), at(k - first)]
            for i in range(j, blocks):
                tile(i, j)[...] -= mm(tile(i, k)[...].astype(BF16), low, NT)


def factor_kernel(size, quick, _, __, mid, packed, diag, low_ref, inv_ref, rest, token, block):
    blocks = mid.shape[0] // size
    cut = blocks // 2
    at = lambda k: pl.ds(k * size, size)

    def tile(i, j):
        return rest.at[at(i - cut), at(j - cut)] if j >= cut else block.at[at(i), at(j)]

    token[...] = jnp.zeros_like(token)
    for k in range(blocks):
        for j in range(k, blocks):
            own = packed[at(k), at(j)].astype(F32)
            if j == k:
                row, col = grid_of(size, size)
                own = jnp.where(col > row, own, 0.0)
                own = own + own.T + jnp.where(col == row, diag[:, at(k)], 0.0)
            else:
                own = own.T
            tile(j, k)[...] = own - mm(mid[at(j), :], mid[at(k), :], NT)
    eliminate(size, quick, tile, low_ref, inv_ref, 0, 0, cut, blocks)


def finish_kernel(size, quick, _, __, rest, low_ref, inv_ref, token, block):
    at = lambda k: pl.ds(k * size, size)
    token[...] = jnp.zeros_like(token)
    block[...] = rest[...]
    blocks = rest.shape[0] // size
    eliminate(size, quick, lambda i, j: block.at[at(i), at(j)], low_ref, inv_ref, 0, 0, blocks, blocks)


def solve_kernel(size, share, _, __, mid, inverse, low_one, inv_one, low_two, inv_two, own_top, own_low, arrows, *refs):
    upper_ref, left_ref, tip_ref, top, rows, solved = refs
    n = mid.shape[0]
    blocks, fixed = n // size, arrows.shape[0] // 2
    cut = blocks // 2
    at = lambda k: pl.ds(k * size, size)

    def low(k):
        if k < cut:
            return low_one[pl.ds((k + 1) * size, n - (k + 1) * size), at(k)]
        return low_two[pl.ds((k + 1 - cut) * size, n - (k + 1) * size), at(k - cut)]

    terms, rest = [], arrows[:fixed]
    for _ in range(3):
        terms.append(rest.astype(BF16).astype(F32))
        rest = rest - terms[-1]
    thin = jnp.concatenate(terms, axis=0).astype(BF16)
    arrow_parts = mm(thin, inverse[...], NT)
    arrow_one = arrow_parts[:fixed] + arrow_parts[fixed : 2 * fixed] + arrow_parts[2 * fixed :]
    for k in range(blocks):
        depth = pl.ds(0, (k + 1) * size)
        top[:, at(k)] = mm(own_top[:, depth], inverse[at(k), depth], NT).astype(BF16)
    rows[:share] = -mm(top[...], mid[...], NT)
    rows[share : 2 * share] = own_low[...].astype(F32)
    arrow_two = arrows[fixed:] - mm(arrow_one.astype(BF16), mid[...], NT)
    rows[2 * share :] = arrow_two
    for k in range(blocks):
        row = rows[:, at(k)].astype(BF16)
        solved[:, at(k)] = mm(row, inv_one[at(k), :] if k < cut else inv_two[at(k - cut), :])
        if k + 1 < blocks:
            rows[:, pl.ds((k + 1) * size, n - (k + 1) * size)] -= mm(row, low(k), NT)
    for k in range(blocks - 2, -1, -1):
        after = solved[:, pl.ds((k + 1) * size, n - (k + 1) * size)]
        solved[:, at(k)] -= mm(after.astype(BF16), low(k))
    upper_ref[...] = solved[: 2 * share].astype(BF16)
    left = (top[...].astype(F32) - mm(upper_ref[:share], mid[...])).astype(BF16)
    for k in range(blocks):
        depth = pl.ds(k * size, n - k * size)
        left_ref[:, at(k)] = mm(left[:, k * size :], inverse[depth, at(k)]).astype(BF16)
    tip_ref[...] = mm(arrow_one, arrow_one, NT, HIGHEST) + mm(solved[2 * share :], arrow_two, NT, HIGHEST)


def product_kernel(share, firsts, offset, signs, places, left, *refs):
    count = len(firsts)
    pieces = refs[:count]
    outs, (whole, sems) = refs[count:-2], refs[-2:]
    started = copies(firsts, share, places, offset, pieces, whole, sems)
    wait(started)
    for i, sign in enumerate(signs):
        product = mm(left[i * share : (i + 1) * share], whole[...], NT)
        product = product if sign > 0 else -product
        outs[2 * i][...] = product
        outs[2 * i + 1][...] = product.astype(BF16)


VMEM = pl.BlockSpec(memory_space=pltpu.VMEM)
ANY = pl.BlockSpec(memory_space=pl.ANY)
SMEM = pl.BlockSpec(memory_space=pltpu.SMEM)


def call(kernel, outs, places, dense, pieces, scratch, flops):
    arrays = [array for array, _ in pieces]
    size = lambda x: x.size * x.dtype.itemsize
    return pl.pallas_call(
        kernel,
        out_shape=outs,
        in_specs=[SMEM] + [VMEM] * len(dense) + [ANY] * len(arrays),
        out_specs=[VMEM] * len(outs),
        scratch_shapes=scratch,
        compiler_params=pltpu.CompilerParams(vmem_limit_bytes=26 << 20),
        cost_estimate=pl.CostEstimate(
            flops=flops, bytes_accessed=sum(map(size, [*dense, *arrays, *outs])), transcendentals=0
        ),
    )(places, *dense, *arrays)


def shards(first_inverse, second_diag, coupling, arrow_rows, tip_block):
    share, n = coupling.shape[2:]
    size = 256 if n % 256 == 0 else 128
    cols = lax.axis_size("col")
    half, fixed = cols // 2, arrow_rows.shape[2]
    core, col = lax.axis_index("tm") % 2, lax.axis_index("col")
    stays = core == col // half
    shape = jax.ShapeDtypeStruct
    dma = pltpu.SemaphoreType.DMA

    row, column = grid_of(share, n, (lax.axis_index("row") * cols + col) * share)
    diag_own = jnp.sum(jnp.where(row == column, second_diag[0], 0), axis=0, keepdims=True)
    packed = jnp.where(column <= row, first_inverse[0], second_diag[0])
    packed = jnp.concatenate([packed, jnp.pad(diag_own, ((0, 15), (0, 0)))], axis=0)
    arrows = move(arrow_rows[0].reshape(2 * fixed, n), swapped)
    both = jnp.concatenate([packed, coupling[0, 1]], axis=0)
    cut = packed.shape[0]
    one = spread(both, cut, begin(both))
    next(one)
    _, gate = one.send(())
    both = jnp.concatenate([coupling[0, 2], coupling[0, 0]], axis=0)
    if gate is not None:
        both, _ = lax.optimization_barrier((both, gate))
    two = spread(both, share, begin(both))
    own = next(two)
    one.send(())
    _, (tops, lows), places = one.send(())
    own_low, own_top = own[:share], own[share:]
    diag = sum(array[share : share + 1].astype(F32) for array, _ in tops)

    firsts = [[f for _, f in p] for p in (tops, lows)]
    count = len(tops)
    whole = pltpu.VMEM((n, n), BF16)
    square_shape, token_shape = shape((n, n), BF16), shape((8, 128), F32)
    mid, packed, inverse, token = call(
        functools.partial(middle_kernel, size, share, firsts),
        [square_shape] * 3 + [token_shape], places, [], tops + lows, [whole, dma((2, count))], n**3,
    )
    (token, arrows), _ = two.send((token, arrows))
    cut = n // size // 2 * size
    rest = n - cut
    low_one, inv_one, block, token = call(
        functools.partial(factor_kernel, size, 3),
        [shape((n, cut), BF16), shape((cut, size), BF16), shape((rest, rest), F32), token_shape],
        places, [token, mid, packed, diag], [], [pltpu.VMEM((n, cut), F32)], 2 * n**3,
    )
    token = two.send(token)
    low_two, inv_two, token = call(
        functools.partial(finish_kernel, size, 3),
        [shape((rest, rest), BF16), shape((rest, size), BF16), token_shape],
        places, [token, block], [], [pltpu.VMEM((rest, rest), F32)], rest**3,
    )
    token, (low_pieces, top_pieces), later = two.send(token)
    solved, left, tip_terms = call(
        functools.partial(solve_kernel, size, share),
        [shape((2 * share, n), BF16), shape((share, n), BF16), shape((fixed, fixed), F32)],
        places, [token, mid, inverse, low_one, inv_one, low_two, inv_two, own_top, own_low, arrows], [],
        [pltpu.VMEM((share, n), BF16)] + [pltpu.VMEM((2 * share + fixed, n), F32)] * 2, 8 * share * n * n,
    )
    tip_half = tip_terms + move(tip_terms, lambda t, r, c: (t, r, (c + half) % cols))
    out = [shape((share, n), F32), shape((share, n), BF16)]
    firsts = [[f for _, f in p] for p in (low_pieces, top_pieces)]
    fill_block, fill_sent, _, handed = call(
        functools.partial(product_kernel, share, firsts[0], 0, (-1, 1)),
        out + out, later, [solved], low_pieces, [whole, dma((count,))], 4 * share * n * n,
    )
    incoming = move(handed, handed_to)
    fill_far = move(fill_sent, swapped)
    own_update, update_sent = call(
        functools.partial(product_kernel, share, firsts[1], count, (1,)),
        out, later, [left], top_pieces, [whole, dma((count,))], 2 * share * n * n,
    )
    update_far = move(update_sent, swapped)
    if lax.axis_size("tm") == 4:
        tip_total = tip_half + move(tip_half, lambda t, r, c: (t ^ 2, r, c))
    else:
        tip_total = lax.psum(jnp.where(core == 0, tip_half, 0.0), "tm")
    fill_block = jnp.where(stays, fill_block, fill_far.astype(F32))
    update = jnp.where(stays, own_update, update_far.astype(F32)) + incoming.astype(F32)
    return (update[None], fill_block[None], tip_block - tip_total)


def solution(mesh):
    return jax.shard_map(
        shards,
        mesh=mesh,
        in_specs=(
            P("tm", ("row", "col"), None),
            P("tm", ("row", "col"), None),
            P("tm", None, ("row", "col"), None),
            P("tm", None, None, None),
            P(),
        ),
        out_specs=(P("tm", ("row", "col"), None), P("tm", ("row", "col"), None), P()),
        check_vma=False,
    )
```
